512 devices in a mesh: seq: 64 (over y, z), head: 8 (over x, core).
Axes of the slice: x: 4, y: 4, z: 16, core: 2. Of those that a mesh axis runs over, the one named last changes fastest.
Arguments:
- queries: bfloat16 [32768, 4096], P(('seq', 'head')), may hold values from -8 to 8
- key_rows: bfloat16 [32768, 4096], P(('seq', 'head')), may hold values from -8 to 8
- value_rows: bfloat16 [32768, 4096], P(('seq', 'head')), may hold values from -8 to 8
- cotangent: bfloat16 [32768, 4096], P(('seq', 'head')), may hold values from -12 to 12
Outputs:
- attended: bfloat16 [32768, 4096], P(('seq', 'head'))
- grad_queries: bfloat16 [32768, 4096], P(('seq', 'head'))
- grad_keys: bfloat16 [32768, 4096], P(('seq', 'head'))
- grad_values: bfloat16 [32768, 4096], P(('seq', 'head'))
The draws below stay inside these ranges and needn't reach their ends.
All inputs are finite; a program needn't handle non-finite values.
Results may differ from the reference program's by a relative error of at most 0.012.
Values may be sent and summed in bfloat16 or wider, within the bound.
No kernel may reach another device: no remote copies, remote signals or barrier semaphores. Data moves between devices by JAX's collectives and lax.ppermute only.
A program may use at most 128 MiB of HBM per device.

```python
import math
import jax
import jax.numpy as jnp
from jax import lax

HEADS = 32
HEAD_DIM = 128
D = 4096
BLOCK = 256
TOKENS = 32768


def rough_smooth(key, rough_scale, smooth_scale):
    level_count = (TOKENS // BLOCK).bit_length() - 1
    field_rows = jax.random.normal(jax.random.fold_in(key, 1), (TOKENS, D), jnp.float32)
    field_rows = field_rows * rough_scale
    for height in range(level_count):
        span_rows = BLOCK * 2 ** height
        coarse_table = jax.random.normal(jax.random.fold_in(key, 100 + height), (TOKENS // span_rows, D), jnp.float32)
        field_rows = (field_rows.reshape(TOKENS // span_rows, span_rows, D) + coarse_table[:, None, :] * (smooth_scale / math.sqrt(level_count))).reshape(TOKENS, D)
    return jnp.clip(field_rows, -8.0, 8.0)


def draw_queries(key, part):
    field_rows = rough_smooth(jax.random.fold_in(key, 11), 1.13, 0.85)
    return field_rows.astype(jnp.bfloat16)


def draw_key_rows(key, part):
    field_rows = rough_smooth(jax.random.fold_in(key, 12), 1.13, 0.85)
    return field_rows.astype(jnp.bfloat16)


def draw_value_rows(key, part):
    return rough_smooth(jax.random.fold_in(key, 13), 0.8, 0.6).astype(jnp.bfloat16)


def block_scale(key, extent, cuts, low, top_value):
    factor_of, own = 1.0, jax.random.fold_in(key, 6)
    for axis_at, blocks in cuts:
        heights = jnp.exp(jax.random.uniform(jax.random.fold_in(own, axis_at), (blocks,), jnp.float32, low / len(cuts), top_value / len(cuts)))
        factor_of = factor_of * jnp.repeat(heights, extent[axis_at] // blocks).reshape([-1 if axis == axis_at else 1 for axis in range(len(extent))])
    return factor_of


def centred(stream_key, dims, scale, reach, pieces=(), held_as=jnp.bfloat16):
    values = scale * jax.random.normal(stream_key, dims, jnp.float32)
    if pieces:
        values = values * block_scale(stream_key, dims, pieces, -0.22, 0.18)
    return jnp.clip(values, -reach, reach).astype(held_as)


def setup_inputs(seed: int = 0) -> dict:
    key_list = jax.random.split(jax.random.key(seed), 5)
    queries = draw_queries(jax.random.fold_in(key_list[4], 71), 0)
    key_rows = draw_key_rows(jax.random.fold_in(key_list[4], 71), 0)
    value_rows = draw_value_rows(jax.random.fold_in(key_list[4], 71), 0)
    cotangent = centred(key_list[3], (TOKENS, D), 2.0, 12.0, ((0, 512),))
    return {"queries": queries, "key_rows": key_rows, "value_rows": value_rows, "cotangent": cotangent}


fill_low = -1e+30
highest = lax.Precision.HIGHEST

def halve_rows(matrix):
    return ((matrix[0::2].astype(jnp.float32) + matrix[1::2].astype(jnp.float32)) * 0.5).astype(jnp.bfloat16)

def swap_pairs(matrix, block_rows):
    pair_count = matrix.shape[0] // block_rows
    return matrix.reshape(pair_count // 2, 2, block_rows, matrix.shape[1])[:, ::-1].reshape(matrix.shape)

def frozen(matrix):
    return lax.optimization_barrier(matrix.astype(jnp.bfloat16)).astype(jnp.float32)

def descend(grads):
    running = grads[-1]
    for height in range(len(grads) - 1, 0, -1):
        running = grads[height - 1] + jnp.repeat(running * 0.5, 2, axis=0)
    return running

def one_head(inputs):
    head_query, head_keys, head_values, head_grad = inputs
    token_count, head_dim = head_query.shape
    block_rows = BLOCK
    block_count = token_count // block_rows
    level_count = block_count.bit_length() - 2
    score_scale = 1.0 / math.sqrt(head_dim)
    query_levels = [head_query]
    key_levels = [head_keys]
    value_levels = [head_values]
    for height in range(level_count):
        query_levels.append(halve_rows(query_levels[-1]))
        key_levels.append(halve_rows(key_levels[-1]))
        value_levels.append(halve_rows(value_levels[-1]))

    def windows(matrix):
        padded = jnp.pad(matrix, ((block_rows, block_rows), (0, 0))).reshape(block_count + 2, block_rows, head_dim)
        return jnp.concatenate([padded[:-2], padded[1:-1], padded[2:]], axis=1).astype(jnp.float32)

    def unwindow(grad_win):
        folded = jnp.pad(grad_win[:, :block_rows], ((0, 2), (0, 0), (0, 0)))
        folded = folded + jnp.pad(grad_win[:, block_rows:2 * block_rows], ((1, 1), (0, 0), (0, 0)))
        folded = folded + jnp.pad(grad_win[:, 2 * block_rows:], ((2, 0), (0, 0), (0, 0)))
        return folded[1:-1].reshape(token_count, head_dim)
    key_win = windows(head_keys)
    value_win = windows(head_values)
    query_blk = head_query.astype(jnp.float32).reshape(block_count, block_rows, head_dim)
    grad_f32 = head_grad.astype(jnp.float32)
    grad_blk = grad_f32.reshape(block_count, block_rows, head_dim)
    block_index = jnp.arange(block_count)
    columns = jnp.arange(3 * block_rows)
    valid_mask = (((columns[None, :] >= block_rows) | (block_index[:, None] > 0)) & ((columns[None, :] < 2 * block_rows) | (block_index[:, None] < block_count - 1)))[:, None, :]
    near_scores = jnp.einsum('bid,bjd->bij', query_blk, key_win, precision=highest) * score_scale
    row_max = lax.optimization_barrier(jnp.max(jnp.where(valid_mask, near_scores, fill_low), axis=2)).reshape(token_count)
    levels = []
    for height in range(1, level_count + 1):
        repeat = 2 ** height
        pair_count = token_count // (repeat * block_rows)
        key_blk = swap_pairs(key_levels[height], block_rows).astype(jnp.float32).reshape(pair_count, block_rows, head_dim)
        value_blk = swap_pairs(value_levels[height], block_rows).astype(jnp.float32).reshape(pair_count, block_rows, head_dim)
        coarse_query = query_levels[height].astype(jnp.float32).reshape(pair_count, block_rows, head_dim)
        coarse_scores = jnp.einsum('crd,cjd->crj', coarse_query, key_blk, precision=highest) * score_scale
        row_max = jnp.maximum(row_max, jnp.repeat(lax.optimization_barrier(jnp.max(coarse_scores, axis=2)).reshape(-1), repeat))
        levels.append((height, pair_count, key_blk, value_blk, coarse_query, coarse_scores))
    near_weights = jnp.where(valid_mask, jnp.exp(near_scores - row_max.reshape(block_count, block_rows, 1)), 0.0)
    totals = lax.optimization_barrier(jnp.sum(near_weights, axis=2)).reshape(token_count)
    numerator = jnp.einsum('bij,bjd->bid', frozen(near_weights), value_win, precision=highest).reshape(token_count, head_dim)
    level_terms = []
    for height, pair_count, key_blk, value_blk, coarse_query, coarse_scores in levels:
        repeat = 2 ** height
        coarse_max = lax.optimization_barrier(jnp.min(row_max.reshape(-1, repeat), axis=1))
        coarse_weights = 2.0 ** height * jnp.exp(coarse_scores - coarse_max.reshape(pair_count, block_rows, 1))
        rescale = jnp.exp(jnp.repeat(coarse_max, repeat) - row_max)
        totals = totals + rescale * jnp.repeat(lax.optimization_barrier(jnp.sum(coarse_weights, axis=2)).reshape(-1), repeat)
        coarse_part = jnp.einsum('crj,cjd->crd', frozen(coarse_weights), value_blk, precision=highest).reshape(-1, head_dim)
        numerator = numerator + jnp.repeat(coarse_part, repeat, axis=0) * rescale[:, None]
        level_terms.append((coarse_weights, rescale))
    attended_f = numerator / totals[:, None]
    delta_rows = lax.optimization_barrier(jnp.sum(grad_f32 * attended_f, axis=1))
    near_share = near_weights / totals.reshape(block_count, block_rows, 1)
    near_prod = jnp.einsum('bid,bjd->bij', grad_blk, value_win, precision=highest)
    near_grad = frozen(near_share * (near_prod - delta_rows.reshape(block_count, block_rows, 1)) * score_scale)
    query_grads = [jnp.einsum('bij,bjd->bid', near_grad, key_win, precision=highest).reshape(token_count, head_dim)]
    key_grads = [unwindow(jnp.einsum('bij,bid->bjd', near_grad, query_blk, precision=highest))]
    value_grads = [unwindow(jnp.einsum('bij,bid->bjd', frozen(near_share), grad_blk, precision=highest))]
    for (height, pair_count, key_blk, value_blk, coarse_query, coarse_scores), (coarse_weights, rescale) in zip(levels, level_terms):
        repeat = 2 ** height
        scaled = rescale / totals
        pooled = lax.optimization_barrier(jnp.sum((grad_f32 * scaled[:, None]).reshape(-1, repeat, head_dim), axis=1))
        pooled_delta = lax.optimization_barrier(jnp.sum((delta_rows * scaled).reshape(-1, repeat), axis=1))
        pooled_blk = pooled.reshape(pair_count, block_rows, head_dim)
        grad_prod = jnp.einsum('crd,cjd->crj', pooled_blk, value_blk, precision=highest)
        coarse_grad = frozen(coarse_weights * (grad_prod - pooled_delta.reshape(pair_count, block_rows, 1)) * score_scale)
        query_grads.append(jnp.einsum('crj,cjd->crd', coarse_grad, key_blk, precision=highest).reshape(-1, head_dim))
        key_part = jnp.einsum('crj,crd->cjd', coarse_grad, coarse_query, precision=highest).reshape(-1, head_dim)
        value_part = jnp.einsum('crj,crd->cjd', frozen(coarse_weights), pooled_blk, precision=highest).reshape(-1, head_dim)
        key_grads.append(swap_pairs(key_part, block_rows))
        value_grads.append(swap_pairs(value_part, block_rows))
    return (attended_f.astype(jnp.bfloat16), descend(query_grads).astype(jnp.bfloat16), descend(key_grads).astype(jnp.bfloat16), descend(value_grads).astype(jnp.bfloat16))

def split_heads(matrix):
    return jnp.transpose(matrix.reshape(matrix.shape[0], HEADS, HEAD_DIM), (1, 0, 2))

def join_heads(stacked):
    return jnp.transpose(stacked, (1, 0, 2)).reshape(stacked.shape[1], HEADS * HEAD_DIM)

def reference(queries, key_rows, value_rows, cotangent):
    results = lax.map(one_head, (split_heads(queries), split_heads(key_rows), split_heads(value_rows), split_heads(cotangent)))
    return (join_heads(results[0]), join_heads(results[1]), join_heads(results[2]), join_heads(results[3]))
```

```python
import math

import jax
import jax.numpy as jnp
from jax import lax
from jax.experimental import pallas as pl
from jax.experimental.pallas import tpu as pltpu
from jax.sharding import Mesh, PartitionSpec as P

HD = 128
BLOCK = 256
LEVELS = 6
NEAR = 3 * BLOCK
SCALE = 1.0 / math.sqrt(HD)
FILL = -1e30
f32 = jnp.float32
bf16 = jnp.bfloat16

ROWS = 2048
CHUNK_BLOCKS = ROWS // BLOCK
COUNT = [ROWS >> l for l in range(LEVELS + 1)]
OFF = [0, 0, 1024, 1536, 1792, 1920, 1984]
COARSE_ROWS = 2016
SIB = [0, 0, 1024, 1536, 1792, 2048, 2304]
SIB_ROWS = 2560

VMEM = pl.BlockSpec(memory_space=pltpu.VMEM)
SMEM = pl.BlockSpec(memory_space=pltpu.SMEM)


def nn(a, b):
    return lax.dot_general(a, b, (((1,), (0,)), ((), ())), preferred_element_type=f32)


def nt(a, b):
    return lax.dot_general(a, b, (((1,), (1,)), ((), ())), preferred_element_type=f32)


def tn(a, b):
    return lax.dot_general(a, b, (((0,), (0,)), ((), ())), preferred_element_type=f32)


def tile(x, n):
    return jnp.concatenate([x] * n, axis=1)


def spread(x):
    return jnp.broadcast_to(x, (x.shape[0], HD))


def pooler(n):
    row = lax.broadcasted_iota(jnp.int32, (n, 2 * n), 0)
    col = lax.broadcasted_iota(jnp.int32, (n, 2 * n), 1)
    return jnp.where(col // 2 == row, 0.5, 0.0).astype(bf16)


def coarsen(x):
    return nn(pooler(x.shape[0] // 2), x).astype(bf16)


def rep(x, tmp):
    n = x.shape[0]
    tmp[pl.ds(0, n, stride=2), :] = x
    tmp[pl.ds(1, n, stride=2), :] = x
    return tmp[0 : 2 * n, :]


def rep_pair(x, tmp_a, tmp_b):
    return jnp.concatenate([rep(x[:, :HD], tmp_a), rep(x[:, HD:], tmp_b)], axis=1)


def pair_sum(x, tmp):
    n = x.shape[0] // 2
    tmp[0 : 2 * n, :] = x
    return tmp[pl.ds(0, n, stride=2), :] + tmp[pl.ds(1, n, stride=2), :]


def pack_kernel(a_ref, b_ref, o_ref):
    for h in range(o_ref.shape[0]):
        o_ref[h, :, 0:HD] = a_ref[:, h * HD : (h + 1) * HD]
        o_ref[h, :, HD : 2 * HD] = b_ref[:, h * HD : (h + 1) * HD]


def unpack_kernel(x_ref, a_ref, b_ref):
    for h in range(x_ref.shape[0]):
        a_ref[:, h * HD : (h + 1) * HD] = x_ref[h, :, 0:HD]
        b_ref[:, h * HD : (h + 1) * HD] = x_ref[h, :, HD : 2 * HD]


def levels_kernel(kv_ref, l1_ref, l2_ref, l4_ref, up_ref, down_ref):
    half = BLOCK // 2
    for b in range(8):
        l1_ref[b * half : (b + 1) * half, :] = coarsen(kv_ref[b * BLOCK : (b + 1) * BLOCK, :])
    for b in range(4):
        l2_ref[b * half : (b + 1) * half, :] = coarsen(l1_ref[b * BLOCK : (b + 1) * BLOCK, :])
    for b in range(2):
        l3 = coarsen(l2_ref[b * BLOCK : (b + 1) * BLOCK, :])
        up_ref[BLOCK + b * half : BLOCK + (b + 1) * half, :] = l3
        down_ref[BLOCK + b * half : BLOCK + (b + 1) * half, :] = l3
    l4_ref[...] = coarsen(up_ref[BLOCK : 2 * BLOCK, :])
    up_ref[0:BLOCK, :] = kv_ref[ROWS - BLOCK : ROWS, :]
    down_ref[0:BLOCK, :] = kv_ref[0:BLOCK, :]


def group_kernel(c_ref, l4_ref, before_ref, after_ref, z2_ref, z3_ref, g5_ref, g6_ref):
    even = c_ref[0] % 2 == 0
    l3 = jnp.where(even, after_ref[BLOCK : 2 * BLOCK, :], before_ref[BLOCK : 2 * BLOCK, :])
    g5_ref[0:64, :] = coarsen(l4_ref[...])
    g5_ref[64:128, :] = coarsen(coarsen(l3))
    g5_ref[128:192, :] = coarsen(z2_ref[...])
    g5_ref[192:256, :] = coarsen(z3_ref[...])
    g6_ref[...] = coarsen(g5_ref[...])


def main_kernel(
    c_ref, kv_ref, qg_ref, l1_ref, l2_ref, before_ref, after_ref, z2_ref, z3_ref, y1_ref, y2_ref, y3_ref,
    ag_ref, d_ref, ups_ref, downs_ref, g3_ref, g4_ref, t1_ref, t2_ref, t3_ref,
    kx, gkx, qc, sib, gs, w_s, u_s, s_s, acc_s, e_s, po_s, pd_s, gq_s, gq0, tmp,
):
    c = c_ref[0]
    half = BLOCK // 2
    even = c % 2 == 0

    kx[0:BLOCK, :] = before_ref[0:BLOCK, :]
    kx[BLOCK : BLOCK + ROWS, :] = kv_ref[...]
    kx[BLOCK + ROWS :, :] = after_ref[0:BLOCK, :]
    gkx[...] = jnp.zeros_like(gkx)
    for b in range(4):
        sib[SIB[1] + b * BLOCK : SIB[1] + (b + 1) * BLOCK, :] = l1_ref[(b ^ 1) * BLOCK : ((b ^ 1) + 1) * BLOCK, :]
    for b in range(2):
        sib[SIB[2] + b * BLOCK : SIB[2] + (b + 1) * BLOCK, :] = l2_ref[(b ^ 1) * BLOCK : ((b ^ 1) + 1) * BLOCK, :]
    sib[SIB[3] : SIB[3] + BLOCK, :] = jnp.where(
        even, after_ref[BLOCK : 2 * BLOCK, :], before_ref[BLOCK : 2 * BLOCK, :]
    )
    sib[SIB[4] : SIB[4] + half, :] = z2_ref[...]
    sib[SIB[4] + half : SIB[4] + BLOCK, :] = z3_ref[...]
    sib[SIB[5] : SIB[5] + BLOCK, :] = y1_ref[...]
    sib[SIB[6] : SIB[6] + half, :] = y2_ref[...]
    sib[SIB[6] + half : SIB[6] + BLOCK, :] = y3_ref[...]

    for b in range(8):
        qc[b * half : (b + 1) * half, :] = coarsen(qg_ref[b * BLOCK : (b + 1) * BLOCK, 0:HD])
    for l in range(2, LEVELS + 1):
        n = min(COUNT[l], half)
        for b in range(COUNT[l] // n):
            src = OFF[l - 1] + 2 * b * n
            qc[OFF[l] + b * n : OFF[l] + (b + 1) * n, :] = coarsen(qc[src : src + 2 * n, :])

    def level_down(l, r0, n, s0, p0):
        rows = pl.ds(r0, n)
        kvs = sib[pl.ds(s0, BLOCK), :]
        scores = nt(qc[rows, :], kvs[:, :HD]) * SCALE
        u = spread(jnp.max(scores, axis=1, keepdims=True))
        if l < LEVELS:
            parent = pl.ds(p0, n // 2)
            pu = rep(u_s[parent, :], tmp.at[0])
            u = jnp.maximum(u, pu)
            e = jnp.exp(pu - u)
            e_s[rows, :] = e
        weights = jnp.exp(scores - tile(u, 2)) * (2.0**l)
        total = spread(jnp.sum(weights, axis=1, keepdims=True))
        acc = nn(weights.astype(bf16), kvs[:, HD:])
        if l < LEVELS:
            total = total + e * rep(s_s[parent, :], tmp.at[1])
            acc = acc + e * rep(acc_s[parent, :], tmp.at[2])
        w_s[rows, :] = weights
        u_s[rows, :] = u
        s_s[rows, :] = total
        acc_s[rows, :] = acc

    def level_up(l, r0, n, s0, p0):
        rows = pl.ds(r0, n)
        kvs = sib[pl.ds(s0, BLOCK), :]
        po = po_s[rows, :]
        pd = pd_s[rows, :]
        high = po.astype(bf16)
        low = (po - high.astype(f32)).astype(bf16)
        parts = jnp.concatenate([high, low], axis=1)
        prod = nt(parts, tile(kvs[:, HD:], 2))
        weights = w_s[rows, :]
        grads = (weights * (prod - tile(pd, 2)) * SCALE).astype(bf16)
        gq_s[rows, :] = nn(grads, kvs[:, :HD])
        gs[pl.ds(s0, BLOCK), 0:HD] = tn(grads, qc[rows, :])
        gv = tn(weights.astype(bf16), parts)
        gs[pl.ds(s0, BLOCK), HD : 2 * HD] = gv[:, :HD] + gv[:, HD:]
        if l < LEVELS:
            e = e_s[rows, :]
            parent = pl.ds(p0, n // 2)
            po_s[parent, :] = pair_sum(e * po, tmp.at[0])
            pd_s[parent, :] = pair_sum(e * pd, tmp.at[1])

    def each_block(step, l):
        def body(b, carry):
            step(
                l,
                pl.multiple_of(OFF[l] + b * BLOCK, BLOCK),
                BLOCK,
                pl.multiple_of(SIB[l] + b * BLOCK, BLOCK),
                pl.multiple_of(OFF[l + 1] + b * half, half),
            )
            return carry

        lax.fori_loop(0, COUNT[l] // BLOCK, body, 0)

    for l in range(LEVELS, 2, -1):
        level_down(l, OFF[l], COUNT[l], SIB[l], OFF[l + 1] if l < LEVELS else 0)
    each_block(level_down, 2)
    each_block(level_down, 1)

    def near(b, carry):
        r = pl.multiple_of(b * BLOCK, BLOCK)
        rows = pl.ds(r, BLOCK)
        window = pl.ds(r, NEAR)
        coarse = pl.ds(pl.multiple_of(b * half, half), half)
        q = qg_ref[rows, 0:HD]
        g = qg_ref[rows, HD : 2 * HD]
        k_win = kx[window, 0:HD]
        v_win = kx[window, HD : 2 * HD]
        column = lax.broadcasted_iota(jnp.int32, (1, NEAR), 1)
        first = jnp.logical_and(c == 0, b == 0)
        last = jnp.logical_and(c == 15, b == CHUNK_BLOCKS - 1)
        low = jnp.where(first, BLOCK, 0)
        high = jnp.where(last, 2 * BLOCK, NEAR)
        bias = jnp.where(jnp.logical_and(column >= low, column < high), 0.0, FILL)
        scores = nt(q, k_win) * SCALE + bias
        pu = rep(u_s[coarse, :], tmp.at[0])
        m = jnp.maximum(spread(jnp.max(scores, axis=1, keepdims=True)), pu)
        e = jnp.exp(pu - m)
        weights = jnp.exp(scores - tile(m, 6))
        totals = spread(jnp.sum(weights, axis=1, keepdims=True)) + e * rep(s_s[coarse, :], tmp.at[1])
        numerator = nn(weights.astype(bf16), v_win) + e * rep(acc_s[coarse, :], tmp.at[2])
        inverse = 1.0 / totals
        attended = numerator * inverse
        ag_ref[rows, 0:HD] = attended.astype(bf16)
        gf = g.astype(f32)
        delta = spread(jnp.sum(gf * attended, axis=1, keepdims=True))
        shares = weights * tile(inverse, 6)
        prod = nt(g, v_win)
        grads = (shares * (prod - tile(delta, 6)) * SCALE).astype(bf16)
        gq0[rows, :] = nn(grads, k_win)
        gkx[window, 0:HD] += tn(grads, q)
        gkx[window, HD : 2 * HD] += tn(shares.astype(bf16), g)
        scaled = e * inverse
        po_s[coarse, :] = pair_sum(scaled * gf, tmp.at[3])
        pd_s[coarse, :] = pair_sum(scaled * delta, tmp.at[4])
        return carry

    lax.fori_loop(0, CHUNK_BLOCKS, near, 0)

    each_block(level_up, 1)
    each_block(level_up, 2)
    for l in range(3, LEVELS + 1):
        level_up(l, OFF[l], COUNT[l], SIB[l], OFF[l + 1] if l < LEVELS else 0)

    for l in range(LEVELS - 1, 0, -1):
        n = min(COUNT[l], BLOCK)
        for b in range(COUNT[l] // n):
            src = OFF[l + 1] + b * (n // 2)
            rows = slice(OFF[l] + b * n, OFF[l] + (b + 1) * n)
            gq_s[rows, :] += rep(gq_s[src : src + n // 2, :] * 0.5, tmp.at[b % 5])
    for j in range(4):
        own = gs.at[SIB[1] + (j ^ 1) * BLOCK : SIB[1] + ((j ^ 1) + 1) * BLOCK]
        i = j // 2
        above = SIB[2] + (i ^ 1) * BLOCK + (j % 2) * half
        own[...] += rep_pair(gs[above : above + half, :] * 0.5, tmp.at[0], tmp.at[1])

    def finish(b, carry):
        rows = pl.ds(pl.multiple_of(b * BLOCK, BLOCK), BLOCK)
        coarse = pl.ds(pl.multiple_of(b * half, half), half)
        ag_ref[rows, HD : 2 * HD] = (gq0[rows, :] + rep(gq_s[coarse, :] * 0.5, tmp.at[0])).astype(bf16)
        j = b // 2
        src = pl.multiple_of(SIB[1] + (j + 1 - 2 * (j % 2)) * BLOCK + (b % 2) * half, half)
        own = pl.ds(pl.multiple_of((b + 1) * BLOCK, BLOCK), BLOCK)
        d_ref[rows, :] = gkx[own, :] + rep_pair(gs[pl.ds(src, half), :] * 0.5, tmp.at[1], tmp.at[2])
        return carry

    lax.fori_loop(0, CHUNK_BLOCKS, finish, 0)
    downs_ref[...] = gkx[0:BLOCK, :].astype(bf16)
    ups_ref[...] = gkx[BLOCK + ROWS :, :].astype(bf16)
    g3_ref[...] = gs[SIB[3] : SIB[3] + BLOCK, :]
    g4_ref[...] = gs[SIB[4] : SIB[4] + BLOCK, :]
    t1_ref[...] = gs[SIB[5] : SIB[5] + BLOCK, :].astype(bf16)
    t2_ref[...] = gs[SIB[6] : SIB[6] + half, :].astype(bf16)
    t3_ref[...] = gs[SIB[6] + half : SIB[6] + BLOCK, :].astype(bf16)


def fold_kernel(
    ups_ref, downs_ref, g3_ref, g4_ref, r1_ref, r2_ref, r3_ref, up_ref, down_ref, z2_ref, z3_ref, own_ref, tmp
):
    def rep2(x):
        return rep_pair(x * 0.5, tmp.at[0], tmp.at[1])

    g6 = r2_ref[...].astype(f32) + r3_ref[...].astype(f32)
    g5 = r1_ref[...].astype(f32) + rep2(g6)
    own_ref[...] = g5[0:64, :]
    l3 = (g3_ref[...] + rep2(rep2(g5[64:128, :]))).astype(bf16)
    up_ref[0:BLOCK, :] = ups_ref[...]
    up_ref[BLOCK : 2 * BLOCK, :] = l3
    down_ref[0:BLOCK, :] = downs_ref[...]
    down_ref[BLOCK : 2 * BLOCK, :] = l3
    z2_ref[...] = (g4_ref[0:128, :] + rep2(g5[128:192, :])).astype(bf16)
    z3_ref[...] = (g4_ref[128:256, :] + rep2(g5[192:256, :])).astype(bf16)


def combine_kernel(c_ref, d_ref, before_ref, after_ref, z2_ref, z3_ref, own_ref, o_ref, tmp, a_s, b_s):
    even = c_ref[0] % 2 == 0

    def rep2(x):
        return rep_pair(x * 0.5, tmp.at[0], tmp.at[1])

    l3 = jnp.where(even, after_ref[BLOCK : 2 * BLOCK, :], before_ref[BLOCK : 2 * BLOCK, :])
    g4 = z2_ref[...].astype(f32) + z3_ref[...].astype(f32) + rep2(own_ref[...])
    g3 = l3.astype(f32) + rep2(g4)
    half = BLOCK // 2
    for b in range(2):
        a_s[b * BLOCK : (b + 1) * BLOCK, :] = rep2(g3[b * half : (b + 1) * half, :])
    for b in range(4):
        b_s[b * BLOCK : (b + 1) * BLOCK, :] = rep2(a_s[b * half : (b + 1) * half, :])
    for b in range(8):
        total = d_ref[b * BLOCK : (b + 1) * BLOCK, :] + rep2(b_s[b * half : (b + 1) * half, :])
        if b == 0:
            total = total + before_ref[0:BLOCK, :].astype(f32)
        if b == 7:
            total = total + after_ref[0:BLOCK, :].astype(f32)
        o_ref[b * BLOCK : (b + 1) * BLOCK, :] = total.astype(bf16)


def shape(dtype, *dims):
    return jax.ShapeDtypeStruct(dims, dtype)


def call(kernel, name, out_shape, scalars, args, scratch=(), flops=0):
    nbytes = sum(a.size * a.dtype.itemsize for a in args)
    return pl.pallas_call(
        kernel,
        name=name,
        out_shape=out_shape,
        in_specs=[SMEM] * scalars + [VMEM] * (len(args) - scalars),
        out_specs=jax.tree.map(lambda _: VMEM, out_shape),
        scratch_shapes=list(scratch),
        cost_estimate=pl.CostEstimate(flops=flops, bytes_accessed=2 * nbytes, transcendentals=0),
    )(*args)


def per_device(queries, key_rows, value_rows, cotangent):
    own_rows, width = queries.shape
    heads = width // HD
    peers = heads
    chunk = (lax.axis_index("y") * lax.axis_size("zh") + lax.axis_index("zh")).astype(jnp.int32).reshape(1)

    def pack(a, b, name):
        return call(pack_kernel, name, shape(bf16, heads, own_rows, 2 * HD), 0, (a, b))

    def swap(x):
        return lax.all_to_all(x, ("zl", "h"), split_axis=0, concat_axis=0, tiled=True)

    def shift(x, distance):
        pairs = [(i, i + distance) for i in range(16) if 0 <= i + distance < 16]
        return lax.ppermute(x, ("y", "zh"), pairs)

    def flip(x, axis, bits):
        return lax.ppermute(x, axis, [(i, i ^ bits) for i in range(4)])

    kv = swap(pack(key_rows, value_rows, "pack_kv")).reshape(ROWS, 2 * HD)
    l1, l2, l4, up, down = call(
        levels_kernel,
        "levels",
        (
            shape(bf16, 1024, 2 * HD),
            shape(bf16, 512, 2 * HD),
            shape(bf16, 128, 2 * HD),
            shape(bf16, 2 * BLOCK, 2 * HD),
            shape(bf16, 2 * BLOCK, 2 * HD),
        ),
        0,
        (kv,),
    )
    before, after = shift(up, 1), shift(down, -1)
    z2, z3 = flip(l4, "zh", 2), flip(l4, "zh", 3)
    packed = pack(queries, cotangent, "pack_qg")
    qg = swap(packed).reshape(ROWS, 2 * HD)
    g5, g6 = call(
        group_kernel,
        "group",
        (shape(bf16, BLOCK, 2 * HD), shape(bf16, 128, 2 * HD)),
        1,
        (chunk, l4, before, after, z2, z3),
    )
    y1, y2, y3 = flip(g5, "y", 1), flip(g6, "y", 2), flip(g6, "y", 3)
    coarse = pltpu.VMEM((COARSE_ROWS, HD), f32)
    ag, d, ups, downs, g3, g4, t1, t2, t3 = call(
        main_kernel,
        "attend",
        (
            shape(bf16, ROWS, 2 * HD),
            shape(f32, ROWS, 2 * HD),
            shape(bf16, BLOCK, 2 * HD),
            shape(bf16, BLOCK, 2 * HD),
            shape(f32, BLOCK, 2 * HD),
            shape(f32, BLOCK, 2 * HD),
            shape(bf16, BLOCK, 2 * HD),
            shape(bf16, 128, 2 * HD),
            shape(bf16, 128, 2 * HD),
        ),
        1,
        (chunk, kv, qg, l1, l2, before, after, z2, z3, y1, y2, y3),
        scratch=(
            pltpu.VMEM((ROWS + 2 * BLOCK, 2 * HD), bf16),
            pltpu.VMEM((ROWS + 2 * BLOCK, 2 * HD), f32),
            pltpu.VMEM((COARSE_ROWS, HD), bf16),
            pltpu.VMEM((SIB_ROWS, 2 * HD), bf16),
            pltpu.VMEM((SIB_ROWS, 2 * HD), f32),
            pltpu.VMEM((COARSE_ROWS, 2 * HD), f32),
            coarse,
            coarse,
            coarse,
            coarse,
            coarse,
            coarse,
            coarse,
            pltpu.VMEM((ROWS, HD), f32),
            pltpu.VMEM((5, BLOCK, HD), f32),
        ),
        flops=4_000_000_000,
    )
    out_ag = swap(ag.reshape(peers, own_rows, 2 * HD))
    r1, r2, r3 = flip(t1, "y", 1), flip(t2, "y", 2), flip(t3, "y", 3)
    up, down, z2, z3, own5 = call(
        fold_kernel,
        "fold",
        (
            shape(bf16, 2 * BLOCK, 2 * HD),
            shape(bf16, 2 * BLOCK, 2 * HD),
            shape(bf16, 128, 2 * HD),
            shape(bf16, 128, 2 * HD),
            shape(f32, 64, 2 * HD),
        ),
        0,
        (ups, downs, g3, g4, r1, r2, r3),
        scratch=(pltpu.VMEM((2, BLOCK, HD), f32),),
    )
    before, after = shift(up, 1), shift(down, -1)
    z2, z3 = flip(z2, "zh", 2), flip(z3, "zh", 3)
    gkv = call(
        combine_kernel,
        "combine",
        shape(bf16, ROWS, 2 * HD),
        1,
        (chunk, d, before, after, z2, z3, own5),
        scratch=(
            pltpu.VMEM((2, BLOCK, HD), f32),
            pltpu.VMEM((512, 2 * HD), f32),
            pltpu.VMEM((1024, 2 * HD), f32),
        ),
    )
    out_kv = swap(gkv.reshape(peers, own_rows, 2 * HD))
    pair = (shape(bf16, own_rows, width), shape(bf16, own_rows, width))
    attended, grad_query = call(unpack_kernel, "unpack_ag", pair, 0, (out_ag,))
    grad_key, grad_value = call(unpack_kernel, "unpack_kv", pair, 0, (out_kv,))
    return attended, grad_query, grad_key, grad_value


def solution(mesh):
    grid = Mesh(mesh.devices.reshape(4, 4, 4, 8), ("y", "zh", "zl", "h"))
    spec = P(("y", "zh", "zl", "h"), None)
    return jax.shard_map(
        per_device,
        mesh=grid,
        in_specs=(spec,) * 4,
        out_specs=(spec,) * 4,
        check_vma=False,
    )
```

```python
import math

import jax
import jax.numpy as jnp
from jax import lax
from jax.experimental import pallas as pl
from jax.experimental.pallas import tpu as pltpu
from jax.sharding import Mesh, PartitionSpec as P


HD = 128
BLOCK = 256
LEVELS = 6
NEAR = 3 * BLOCK
SCALE = 1.0 / math.sqrt(HD)
FILL = -1e30
f32 = jnp.float32
bf16 = jnp.bfloat16

ROWS = 2048
CHUNK_BLOCKS = ROWS // BLOCK
COUNT = [ROWS >> l for l in range(LEVELS + 1)]
OFF = [0, 0, 1024, 1536, 1792, 1920, 1984]
COARSE_ROWS = 2016
SIB = [0, 0, 1024, 1536, 1792, 2048, 2304]
SIB_ROWS = 2560

VMEM = pl.BlockSpec(memory_space=pltpu.VMEM)
SMEM = pl.BlockSpec(memory_space=pltpu.SMEM)


def nn(a, b):
    return lax.dot_general(a, b, (((1,), (0,)), ((), ())), preferred_element_type=f32)


def nt(a, b):
    return lax.dot_general(a, b, (((1,), (1,)), ((), ())), preferred_element_type=f32)


def tn(a, b):
    return lax.dot_general(a, b, (((0,), (0,)), ((), ())), preferred_element_type=f32)


def tile(x, n):
    return jnp.concatenate([x] * n, axis=1)


def spread(x):
    return jnp.broadcast_to(x, (x.shape[0], HD))


def pooler(n):
    row = lax.broadcasted_iota(jnp.int32, (n, 2 * n), 0)
    col = lax.broadcasted_iota(jnp.int32, (n, 2 * n), 1)
    return jnp.where(col // 2 == row, 0.5, 0.0).astype(bf16)


def coarsen(x):
    return nn(pooler(x.shape[0] // 2), x).astype(bf16)


def rep(x, tmp):
    n = x.shape[0]
    tmp[pl.ds(0, n, stride=2), :] = x
    tmp[pl.ds(1, n, stride=2), :] = x
    return tmp[0 : 2 * n, :]


def rep_pair(x, tmp_a, tmp_b):
    return jnp.concatenate([rep(x[:, :HD], tmp_a), rep(x[:, HD:], tmp_b)], axis=1)


def pair_sum(x, tmp):
    n = x.shape[0] // 2
    tmp[0 : 2 * n, :] = x
    return tmp[pl.ds(0, n, stride=2), :] + tmp[pl.ds(1, n, stride=2), :]


def pack_kernel(a_ref, b_ref, o_ref):
    for h in range(o_ref.shape[0]):
        o_ref[h, :, 0:HD] = a_ref[:, h * HD : (h + 1) * HD]
        o_ref[h, :, HD : 2 * HD] = b_ref[:, h * HD : (h + 1) * HD]


def unpack_kernel(x_ref, a_ref, b_ref):
    for h in range(x_ref.shape[0]):
        a_ref[:, h * HD : (h + 1) * HD] = x_ref[h, :, 0:HD]
        b_ref[:, h * HD : (h + 1) * HD] = x_ref[h, :, HD : 2 * HD]


def levels_kernel(kv_ref, l1_ref, l2_ref, l3_ref, l4_ref):
    half = BLOCK // 2
    for b in range(8):
        l1_ref[b * half : (b + 1) * half, :] = coarsen(kv_ref[b * BLOCK : (b + 1) * BLOCK, :])
    for b in range(4):
        l2_ref[b * half : (b + 1) * half, :] = coarsen(l1_ref[b * BLOCK : (b + 1) * BLOCK, :])
    for b in range(2):
        l3_ref[b * half : (b + 1) * half, :] = coarsen(l2_ref[b * BLOCK : (b + 1) * BLOCK, :])
    l4_ref[...] = coarsen(l3_ref[...])


def group_kernel(l4_ref, z1_ref, z2_ref, z3_ref, o_ref):
    parts = (l4_ref[...], coarsen(z1_ref[...]), z2_ref[...], z3_ref[...])
    for k, part in enumerate(parts):
        o_ref[k * 64 : (k + 1) * 64, :] = coarsen(part)


def main_kernel(
    c_ref, kv_ref, qg_ref, l1_ref, l2_ref, before_ref, after_ref, z1_ref, z2_ref, z3_ref, y_ref,
    ag_ref, d_ref, up_ref, down_ref, w1_ref, w2_ref, t1_ref, t2_ref, t3_ref,
    kx, gkx, qc, sib, gs, w_s, u_s, s_s, acc_s, e_s, po_s, pd_s, gq_s, gq0, tmp,
):
    c = c_ref[0]
    half = BLOCK // 2

    kx[0:BLOCK, :] = before_ref[...]
    kx[BLOCK : BLOCK + ROWS, :] = kv_ref[...]
    kx[BLOCK + ROWS :, :] = after_ref[...]
    gkx[...] = jnp.zeros_like(gkx)
    for b in range(4):
        sib[SIB[1] + b * BLOCK : SIB[1] + (b + 1) * BLOCK, :] = l1_ref[(b ^ 1) * BLOCK : ((b ^ 1) + 1) * BLOCK, :]
    for b in range(2):
        sib[SIB[2] + b * BLOCK : SIB[2] + (b + 1) * BLOCK, :] = l2_ref[(b ^ 1) * BLOCK : ((b ^ 1) + 1) * BLOCK, :]
    sib[SIB[3] : SIB[3] + BLOCK, :] = z1_ref[...]
    sib[SIB[4] : SIB[4] + half, :] = z2_ref[...]
    sib[SIB[4] + half : SIB[4] + BLOCK, :] = z3_ref[...]
    y = c // 4
    sib[SIB[5] : SIB[5] + BLOCK, :] = y_ref[y ^ 1]
    sib[SIB[6] : SIB[6] + half, :] = coarsen(y_ref[y ^ 2])
    sib[SIB[6] + half : SIB[6] + BLOCK, :] = coarsen(y_ref[y ^ 3])

    for b in range(8):
        qc[b * half : (b + 1) * half, :] = coarsen(qg_ref[b * BLOCK : (b + 1) * BLOCK, 0:HD])
    for l in range(2, LEVELS + 1):
        n = min(COUNT[l], half)
        for b in range(COUNT[l] // n):
            src = OFF[l - 1] + 2 * b * n
            qc[OFF[l] + b * n : OFF[l] + (b + 1) * n, :] = coarsen(qc[src : src + 2 * n, :])

    def level_down(l, r0, n, s0, p0):
        rows = pl.ds(r0, n)
        kvs = sib[pl.ds(s0, BLOCK), :]
        scores = nt(qc[rows, :], kvs[:, :HD]) * SCALE
        u = spread(jnp.max(scores, axis=1, keepdims=True))
        if l < LEVELS:
            parent = pl.ds(p0, n // 2)
            pu = rep(u_s[parent, :], tmp.at[0])
            u = jnp.maximum(u, pu)
            e = jnp.exp(pu - u)
            e_s[rows, :] = e
        weights = jnp.exp(scores - tile(u, 2)) * (2.0**l)
        total = spread(jnp.sum(weights, axis=1, keepdims=True))
        acc = nn(weights.astype(bf16), kvs[:, HD:])
        if l < LEVELS:
            total = total + e * rep(s_s[parent, :], tmp.at[1])
            acc = acc + e * rep(acc_s[parent, :], tmp.at[2])
        w_s[rows, :] = weights
        u_s[rows, :] = u
        s_s[rows, :] = total
        acc_s[rows, :] = acc

    def level_up(l, r0, n, s0, p0):
        rows = pl.ds(r0, n)
        kvs = sib[pl.ds(s0, BLOCK), :]
        po = po_s[rows, :]
        pd = pd_s[rows, :]
        high = po.astype(bf16)
        low = (po - high.astype(f32)).astype(bf16)
        parts = jnp.concatenate([high, low], axis=1)
        prod = nt(parts, tile(kvs[:, HD:], 2))
        weights = w_s[rows, :]
        grads = (weights * (prod - tile(pd, 2)) * SCALE).astype(bf16)
        gq_s[rows, :] = nn(grads, kvs[:, :HD])
        gs[pl.ds(s0, BLOCK), 0:HD] = tn(grads, qc[rows, :])
        gv = tn(weights.astype(bf16), parts)
        gs[pl.ds(s0, BLOCK), HD : 2 * HD] = gv[:, :HD] + gv[:, HD:]
        if l < LEVELS:
            e = e_s[rows, :]
            parent = pl.ds(p0, n // 2)
            po_s[parent, :] = pair_sum(e * po, tmp.at[0])
            pd_s[parent, :] = pair_sum(e * pd, tmp.at[1])

    def each_block(step, l):
        def body(b, carry):
            step(
                l,
                pl.multiple_of(OFF[l] + b * BLOCK, BLOCK),
                BLOCK,
                pl.multiple_of(SIB[l] + b * BLOCK, BLOCK),
                pl.multiple_of(OFF[l + 1] + b * half, half),
            )
            return carry

        lax.fori_loop(0, COUNT[l] // BLOCK, body, 0)

    for l in range(LEVELS, 2, -1):
        level_down(l, OFF[l], COUNT[l], SIB[l], OFF[l + 1] if l < LEVELS else 0)
    each_block(level_down, 2)
    each_block(level_down, 1)

    def near(b, carry):
        r = pl.multiple_of(b * BLOCK, BLOCK)
        rows = pl.ds(r, BLOCK)
        window = pl.ds(r, NEAR)
        coarse = pl.ds(pl.multiple_of(b * half, half), half)
        q = qg_ref[rows, 0:HD]
        g = qg_ref[rows, HD : 2 * HD]
        k_win = kx[window, 0:HD]
        v_win = kx[window, HD : 2 * HD]
        column = lax.broadcasted_iota(jnp.int32, (1, NEAR), 1)
        first = jnp.logical_and(c == 0, b == 0)
        last = jnp.logical_and(c == 15, b == CHUNK_BLOCKS - 1)
        low = jnp.where(first, BLOCK, 0)
        high = jnp.where(last, 2 * BLOCK, NEAR)
        bias = jnp.where(jnp.logical_and(column >= low, column < high), 0.0, FILL)
        scores = nt(q, k_win) * SCALE + bias
        pu = rep(u_s[coarse, :], tmp.at[0])
        m = jnp.maximum(spread(jnp.max(scores, axis=1, keepdims=True)), pu)
        e = jnp.exp(pu - m)
        weights = jnp.exp(scores - tile(m, 6))
        totals = spread(jnp.sum(weights, axis=1, keepdims=True)) + e * rep(s_s[coarse, :], tmp.at[1])
        numerator = nn(weights.astype(bf16), v_win) + e * rep(acc_s[coarse, :], tmp.at[2])
        inverse = 1.0 / totals
        attended = numerator * inverse
        ag_ref[rows, 0:HD] = attended.astype(bf16)
        gf = g.astype(f32)
        delta = spread(jnp.sum(gf * attended, axis=1, keepdims=True))
        shares = weights * tile(inverse, 6)
        prod = nt(g, v_win)
        grads = (shares * (prod - tile(delta, 6)) * SCALE).astype(bf16)
        gq0[rows, :] = nn(grads, k_win)
        gkx[window, 0:HD] += tn(grads, q)
        gkx[window, HD : 2 * HD] += tn(shares.astype(bf16), g)
        scaled = e * inverse
        po_s[coarse, :] = pair_sum(scaled * gf, tmp.at[3])
        pd_s[coarse, :] = pair_sum(scaled * delta, tmp.at[4])
        return carry

    lax.fori_loop(0, CHUNK_BLOCKS, near, 0)

    each_block(level_up, 1)
    each_block(level_up, 2)
    for l in range(3, LEVELS + 1):
        level_up(l, OFF[l], COUNT[l], SIB[l], OFF[l + 1] if l < LEVELS else 0)

    for l in range(LEVELS - 1, 0, -1):
        n = min(COUNT[l], BLOCK)
        for b in range(COUNT[l] // n):
            src = OFF[l + 1] + b * (n // 2)
            rows = slice(OFF[l] + b * n, OFF[l] + (b + 1) * n)
            gq_s[rows, :] += rep(gq_s[src : src + n // 2, :] * 0.5, tmp.at[b % 5])
    for j in range(4):
        own = gs.at[SIB[1] + (j ^ 1) * BLOCK : SIB[1] + ((j ^ 1) + 1) * BLOCK]
        i = j // 2
        above = SIB[2] + (i ^ 1) * BLOCK + (j % 2) * half
        own[...] += rep_pair(gs[above : above + half, :] * 0.5, tmp.at[0], tmp.at[1])

    def finish(b, carry):
        rows = pl.ds(pl.multiple_of(b * BLOCK, BLOCK), BLOCK)
        coarse = pl.ds(pl.multiple_of(b * half, half), half)
        ag_ref[rows, HD : 2 * HD] = (gq0[rows, :] + rep(gq_s[coarse, :] * 0.5, tmp.at[0])).astype(bf16)
        j = b // 2
        src = pl.multiple_of(SIB[1] + (j + 1 - 2 * (j % 2)) * BLOCK + (b % 2) * half, half)
        own = pl.ds(pl.multiple_of((b + 1) * BLOCK, BLOCK), BLOCK)
        d_ref[rows, :] = gkx[own, :] + rep_pair(gs[pl.ds(src, half), :] * 0.5, tmp.at[1], tmp.at[2])
        return carry

    lax.fori_loop(0, CHUNK_BLOCKS, finish, 0)
    down_ref[...] = gkx[0:BLOCK, :].astype(bf16)
    up_ref[...] = gkx[BLOCK + ROWS :, :].astype(bf16)
    w1_ref[...] = gs[SIB[3] : SIB[3] + BLOCK, :]
    w2_ref[...] = gs[SIB[4] : SIB[4] + BLOCK, :]
    t1_ref[...] = gs[SIB[5] : SIB[5] + BLOCK, :].astype(bf16)
    t2_ref[...] = gs[SIB[6] : SIB[6] + half, :].astype(bf16)
    t3_ref[...] = gs[SIB[6] + half : SIB[6] + BLOCK, :].astype(bf16)


def fold_kernel(r1_ref, r2_ref, r3_ref, w1_ref, w2_ref, own_ref, z1_ref, z2_ref, z3_ref, tmp):
    def rep2(x):
        return rep_pair(x * 0.5, tmp.at[0], tmp.at[1])

    half = BLOCK // 2
    g5 = r1_ref[...].astype(f32) + rep2(r2_ref[...].astype(f32) + r3_ref[...].astype(f32))
    own_ref[...] = g5[0:64, :]
    z1_ref[...] = (w1_ref[...] + rep2(rep2(g5[64:128, :]))).astype(bf16)
    z2_ref[...] = (w2_ref[0:half, :] + rep2(g5[128:192, :])).astype(bf16)
    z3_ref[...] = (w2_ref[half:BLOCK, :] + rep2(g5[192:256, :])).astype(bf16)


def combine_kernel(d_ref, before_ref, after_ref, z1_ref, z2_ref, z3_ref, own_ref, o_ref, tmp, a_s, b_s):
    def rep2(x):
        return rep_pair(x * 0.5, tmp.at[0], tmp.at[1])

    g4 = z2_ref[...].astype(f32) + z3_ref[...].astype(f32) + rep2(own_ref[...])
    g3 = z1_ref[...].astype(f32) + rep2(g4)
    half = BLOCK // 2
    for b in range(2):
        a_s[b * BLOCK : (b + 1) * BLOCK, :] = rep2(g3[b * half : (b + 1) * half, :])
    for b in range(4):
        b_s[b * BLOCK : (b + 1) * BLOCK, :] = rep2(a_s[b * half : (b + 1) * half, :])
    for b in range(8):
        total = d_ref[b * BLOCK : (b + 1) * BLOCK, :] + rep2(b_s[b * half : (b + 1) * half, :])
        if b == 0:
            total = total + before_ref[...].astype(f32)
        if b == 7:
            total = total + after_ref[...].astype(f32)
        o_ref[b * BLOCK : (b + 1) * BLOCK, :] = total.astype(bf16)


def shape(dtype, *dims):
    return jax.ShapeDtypeStruct(dims, dtype)


def call(kernel, out_shape, scalars, args, scratch=(), flops=0):
    nbytes = sum(a.size * a.dtype.itemsize for a in args)
    return pl.pallas_call(
        kernel,
        out_shape=out_shape,
        in_specs=[SMEM] * scalars + [VMEM] * (len(args) - scalars),
        out_specs=jax.tree.map(lambda _: VMEM, out_shape),
        scratch_shapes=list(scratch),
        cost_estimate=pl.CostEstimate(flops=flops, bytes_accessed=2 * nbytes, transcendentals=0),
    )(*args)


def per_device(queries, key_rows, value_rows, cotangent):
    own_rows, width = queries.shape
    heads = width // HD
    chunk = (lax.axis_index("y") * lax.axis_size("zh") + lax.axis_index("zh")).astype(jnp.int32).reshape(1)
    wide = 2 * HD

    def pack(a, b):
        return call(pack_kernel, shape(bf16, heads, own_rows, wide), 0, (a, b))

    def swap(x):
        return lax.all_to_all(x, ("zl", "h"), split_axis=0, concat_axis=0, tiled=True)

    def shift(x, distance):
        pairs = [(i, i + distance) for i in range(16) if 0 <= i + distance < 16]
        return lax.ppermute(x, ("y", "zh"), pairs)

    def flip(x, axis, bits):
        return lax.ppermute(x, axis, [(i, i ^ bits) for i in range(4)])

    kv = swap(pack(key_rows, value_rows)).reshape(ROWS, wide)
    l1, l2, l3, l4 = call(
        levels_kernel,
        (shape(bf16, 1024, wide), shape(bf16, 512, wide), shape(bf16, 256, wide), shape(bf16, 128, wide)),
        0,
        (kv,),
    )
    z1, z2, z3 = flip(l3, "zh", 1), flip(l4, "zh", 2), flip(l4, "zh", 3)
    before = shift(kv[ROWS - BLOCK :], 1)
    after = shift(kv[:BLOCK], -1)
    qg = swap(pack(queries, cotangent)).reshape(ROWS, wide)
    group = call(group_kernel, shape(bf16, BLOCK, wide), 0, (l4, z1, z2, z3))
    far = lax.all_gather(group, "y")
    coarse = pltpu.VMEM((COARSE_ROWS, HD), f32)
    ag, d, up, down, w1, w2, t1, t2, t3 = call(
        main_kernel,
        (
            shape(bf16, ROWS, wide),
            shape(f32, ROWS, wide),
            shape(bf16, BLOCK, wide),
            shape(bf16, BLOCK, wide),
            shape(f32, BLOCK, wide),
            shape(f32, BLOCK, wide),
            shape(bf16, BLOCK, wide),
            shape(bf16, 128, wide),
            shape(bf16, 128, wide),
        ),
        1,
        (chunk, kv, qg, l1, l2, before, after, z1, z2, z3, far),
        scratch=(
            pltpu.VMEM((ROWS + 2 * BLOCK, wide), bf16),
            pltpu.VMEM((ROWS + 2 * BLOCK, wide), f32),
            pltpu.VMEM((COARSE_ROWS, HD), bf16),
            pltpu.VMEM((SIB_ROWS, wide), bf16),
            pltpu.VMEM((SIB_ROWS, wide), f32),
            pltpu.VMEM((COARSE_ROWS, wide), f32),
            coarse,
            coarse,
            coarse,
            coarse,
            coarse,
            coarse,
            coarse,
            pltpu.VMEM((ROWS, HD), f32),
            pltpu.VMEM((5, BLOCK, HD), f32),
        ),
        flops=4_000_000_000,
    )
    out_ag = swap(ag.reshape(heads, own_rows, wide))
    r1, r2, r3 = flip(t1, "y", 1), flip(t2, "y", 2), flip(t3, "y", 3)
    before = shift(up, 1)
    after = shift(down, -1)
    two = pltpu.VMEM((2, BLOCK, HD), f32)
    own5, w1, w2, w3 = call(
        fold_kernel,
        (shape(f32, 64, wide), shape(bf16, BLOCK, wide), shape(bf16, 128, wide), shape(bf16, 128, wide)),
        0,
        (r1, r2, r3, w1, w2),
        scratch=(two,),
    )
    z1, z2, z3 = flip(w1, "zh", 1), flip(w2, "zh", 2), flip(w3, "zh", 3)
    gkv = call(
        combine_kernel,
        shape(bf16, ROWS, wide),
        0,
        (d, before, after, z1, z2, z3, own5),
        scratch=(two, pltpu.VMEM((512, wide), f32), pltpu.VMEM((1024, wide), f32)),
    )
    out_kv = swap(gkv.reshape(heads, own_rows, wide))
    pair = (shape(bf16, own_rows, width), shape(bf16, own_rows, width))
    attended, grad_query = call(unpack_kernel, pair, 0, (out_ag,))
    grad_key, grad_value = call(unpack_kernel, pair, 0, (out_kv,))
    return attended, grad_query, grad_key, grad_value


def solution(mesh):
    grid = Mesh(mesh.devices.reshape(4, 4, 4, 8), ("y", "zh", "zl", "h"))
    spec = P(("y", "zh", "zl", "h"), None)

    return jax.shard_map(per_device, mesh=grid, in_specs=(spec,) * 4, out_specs=(spec,) * 4, check_vma=False)
```

```python
import math

import jax
import jax.numpy as jnp
from jax import lax
from jax.experimental import pallas as pl
from jax.experimental.pallas import tpu as pltpu
from jax.sharding import Mesh, PartitionSpec as P


HD = 128
BLOCK = 256
LEVELS = 6
NEAR = 3 * BLOCK
SCALE = 1.0 / math.sqrt(HD)
FILL = -1e30
f32 = jnp.float32
bf16 = jnp.bfloat16

ROWS = 2048
CHUNK_BLOCKS = ROWS // BLOCK
COUNT = [ROWS >> l for l in range(LEVELS + 1)]
OFF = [0, 0, 1024, 1536, 1792, 1920, 1984]
COARSE_ROWS = 2016
SIB = [0, 0, 1024, 1536, 1792, 2048, 2304]
SIB_ROWS = 2560

PARTS = 4

VMEM = pl.BlockSpec(memory_space=pltpu.VMEM)
SMEM = pl.BlockSpec(memory_space=pltpu.SMEM)


def nn(a, b):
    return lax.dot_general(a, b, (((1,), (0,)), ((), ())), preferred_element_type=f32)


def nt(a, b):
    return lax.dot_general(a, b, (((1,), (1,)), ((), ())), preferred_element_type=f32)


def tn(a, b):
    return lax.dot_general(a, b, (((0,), (0,)), ((), ())), preferred_element_type=f32)


def tile(x, n):
    return jnp.concatenate([x] * n, axis=1)


def spread(x):
    return jnp.broadcast_to(x, (x.shape[0], HD))


def pooler(n):
    row = lax.broadcasted_iota(jnp.int32, (n, 2 * n), 0)
    col = lax.broadcasted_iota(jnp.int32, (n, 2 * n), 1)
    return jnp.where(col // 2 == row, 0.5, 0.0).astype(bf16)


def coarsen(x):
    return nn(pooler(x.shape[0] // 2), x).astype(bf16)


def rep(x, tmp):
    n = x.shape[0]
    tmp[pl.ds(0, n, stride=2), :] = x
    tmp[pl.ds(1, n, stride=2), :] = x
    return tmp[0 : 2 * n, :]


def rep_pair(x, tmp_a, tmp_b):
    return jnp.concatenate([rep(x[:, :HD], tmp_a), rep(x[:, HD:], tmp_b)], axis=1)


def pair_sum(x, tmp):
    n = x.shape[0] // 2
    tmp[0 : 2 * n, :] = x
    return tmp[pl.ds(0, n, stride=2), :] + tmp[pl.ds(1, n, stride=2), :]


def pack_kernel(a_ref, b_ref, o_ref):
    for h in range(o_ref.shape[0]):
        o_ref[h, :, 0:HD] = a_ref[:, h * HD : (h + 1) * HD]
        o_ref[h, :, HD : 2 * HD] = b_ref[:, h * HD : (h + 1) * HD]


def pack(a, b):
    rows, width = a.shape
    return call(pack_kernel, shape(bf16, width // HD, rows, 2 * HD), 0, (a, b))


def unpack_kernel(x_ref, a_ref, b_ref):
    i = pl.program_id(0)
    n = x_ref.shape[0] // PARTS
    for h in range(n):
        a_ref[:, h * HD : (h + 1) * HD] = x_ref[i * n + h, :, 0:HD]
        b_ref[:, h * HD : (h + 1) * HD] = x_ref[i * n + h, :, HD : 2 * HD]


def unpack(x):
    heads, rows, _ = x.shape
    width = heads * HD
    part = pl.BlockSpec((rows, width // PARTS), lambda i: (0, i))
    return pl.pallas_call(
        unpack_kernel,
        grid=(PARTS,),
        out_shape=(shape(bf16, rows, width), shape(bf16, rows, width)),
        in_specs=[VMEM],
        out_specs=(part, part),
        cost_estimate=pl.CostEstimate(flops=0, bytes_accessed=4 * x.size, transcendentals=0),
    )(pltpu.with_memory_space_constraint(x, pltpu.VMEM))


def levels_kernel(kv_ref, l1_ref, l2_ref, l3_ref, l4_ref):
    half = BLOCK // 2
    for b in range(8):
        l1_ref[b * half : (b + 1) * half, :] = coarsen(kv_ref[b * BLOCK : (b + 1) * BLOCK, :])
    for b in range(4):
        l2_ref[b * half : (b + 1) * half, :] = coarsen(l1_ref[b * BLOCK : (b + 1) * BLOCK, :])
    for b in range(2):
        l3_ref[b * half : (b + 1) * half, :] = coarsen(l2_ref[b * BLOCK : (b + 1) * BLOCK, :])
    l4_ref[...] = coarsen(l3_ref[...])


def group_kernel(l4_ref, z1_ref, z2_ref, z3_ref, o_ref):
    parts = (l4_ref[...], coarsen(z1_ref[...]), z2_ref[...], z3_ref[...])
    for k, part in enumerate(parts):
        o_ref[k * 64 : (k + 1) * 64, :] = coarsen(part)


def main_kernel(
    c_ref, kv_ref, qg_ref, l1_ref, l2_ref, before_ref, after_ref, z1_ref, z2_ref, z3_ref, y_ref,
    ag_ref, d_ref, up_ref, down_ref, w1_ref, w2_ref, t1_ref, t2_ref, t3_ref,
    kx, gkx, qc, sib, gs, w_s, u_s, s_s, acc_s, e_s, po_s, pd_s, gq_s, gq0, tmp,
):
    c = c_ref[0]
    half = BLOCK // 2

    kx[0:BLOCK, :] = before_ref[...]
    kx[BLOCK : BLOCK + ROWS, :] = kv_ref[...]
    kx[BLOCK + ROWS :, :] = after_ref[...]
    gkx[...] = jnp.zeros_like(gkx)
    for b in range(4):
        sib[SIB[1] + b * BLOCK : SIB[1] + (b + 1) * BLOCK, :] = l1_ref[(b ^ 1) * BLOCK : ((b ^ 1) + 1) * BLOCK, :]
    for b in range(2):
        sib[SIB[2] + b * BLOCK : SIB[2] + (b + 1) * BLOCK, :] = l2_ref[(b ^ 1) * BLOCK : ((b ^ 1) + 1) * BLOCK, :]
    sib[SIB[3] : SIB[3] + BLOCK, :] = z1_ref[...]
    sib[SIB[4] : SIB[4] + half, :] = z2_ref[...]
    sib[SIB[4] + half : SIB[4] + BLOCK, :] = z3_ref[...]
    y = c // 4
    sib[SIB[5] : SIB[5] + BLOCK, :] = y_ref[y ^ 1]
    sib[SIB[6] : SIB[6] + half, :] = coarsen(y_ref[y ^ 2])
    sib[SIB[6] + half : SIB[6] + BLOCK, :] = coarsen(y_ref[y ^ 3])

    for b in range(8):
        qc[b * half : (b + 1) * half, :] = coarsen(qg_ref[b * BLOCK : (b + 1) * BLOCK, 0:HD])
    for l in range(2, LEVELS + 1):
        n = min(COUNT[l], half)
        for b in range(COUNT[l] // n):
            src = OFF[l - 1] + 2 * b * n
            qc[OFF[l] + b * n : OFF[l] + (b + 1) * n, :] = coarsen(qc[src : src + 2 * n, :])

    def level_down(l, r0, n, s0, p0):
        rows = pl.ds(r0, n)
        kvs = sib[pl.ds(s0, BLOCK), :]
        scores = nt(qc[rows, :], kvs[:, :HD]) * SCALE
        u = spread(jnp.max(scores, axis=1, keepdims=True))
        if l < LEVELS:
            parent = pl.ds(p0, n // 2)
            pu = rep(u_s[parent, :], tmp.at[0])
            u = jnp.maximum(u, pu)
            e = jnp.exp(pu - u)
            e_s[rows, :] = e
        weights = jnp.exp(scores - tile(u, 2)) * (2.0**l)
        total = spread(jnp.sum(weights, axis=1, keepdims=True))
        acc = nn(weights.astype(bf16), kvs[:, HD:])
        if l < LEVELS:
            total = total + e * rep(s_s[parent, :], tmp.at[1])
            acc = acc + e * rep(acc_s[parent, :], tmp.at[2])
        w_s[rows, :] = weights
        u_s[rows, :] = u
        s_s[rows, :] = total
        acc_s[rows, :] = acc

    def level_up(l, r0, n, s0, p0):
        rows = pl.ds(r0, n)
        kvs = sib[pl.ds(s0, BLOCK), :]
        po = po_s[rows, :]
        pd = pd_s[rows, :]
        high = po.astype(bf16)
        low = (po - high.astype(f32)).astype(bf16)
        parts = jnp.concatenate([high, low], axis=1)
        prod = nt(parts, tile(kvs[:, HD:], 2))
        weights = w_s[rows, :]
        grads = (weights * (prod - tile(pd, 2)) * SCALE).astype(bf16)
        gq_s[rows, :] = nn(grads, kvs[:, :HD])
        gs[pl.ds(s0, BLOCK), 0:HD] = tn(grads, qc[rows, :])
        gv = tn(weights.astype(bf16), parts)
        gs[pl.ds(s0, BLOCK), HD : 2 * HD] = gv[:, :HD] + gv[:, HD:]
        if l < LEVELS:
            e = e_s[rows, :]
            parent = pl.ds(p0, n // 2)
            po_s[parent, :] = pair_sum(e * po, tmp.at[0])
            pd_s[parent, :] = pair_sum(e * pd, tmp.at[1])

    def each_block(step, l):
        def body(b, carry):
            step(
                l,
                pl.multiple_of(OFF[l] + b * BLOCK, BLOCK),
                BLOCK,
                pl.multiple_of(SIB[l] + b * BLOCK, BLOCK),
                pl.multiple_of(OFF[l + 1] + b * half, half),
            )
            return carry

        lax.fori_loop(0, COUNT[l] // BLOCK, body, 0)

    for l in range(LEVELS, 2, -1):
        level_down(l, OFF[l], COUNT[l], SIB[l], OFF[l + 1] if l < LEVELS else 0)
    each_block(level_down, 2)
    each_block(level_down, 1)

    def near(b, carry):
        r = pl.multiple_of(b * BLOCK, BLOCK)
        rows = pl.ds(r, BLOCK)
        window = pl.ds(r, NEAR)
        coarse = pl.ds(pl.multiple_of(b * half, half), half)
        q = qg_ref[rows, 0:HD]
        g = qg_ref[rows, HD : 2 * HD]
        k_win = kx[window, 0:HD]
        v_win = kx[window, HD : 2 * HD]
        column = lax.broadcasted_iota(jnp.int32, (1, NEAR), 1)
        first = jnp.logical_and(c == 0, b == 0)
        last = jnp.logical_and(c == 15, b == CHUNK_BLOCKS - 1)
        low = jnp.where(first, BLOCK, 0)
        high = jnp.where(last, 2 * BLOCK, NEAR)
        bias = jnp.where(jnp.logical_and(column >= low, column < high), 0.0, FILL)
        scores = nt(q, k_win) * SCALE + bias
        pu = rep(u_s[coarse, :], tmp.at[0])
        m = jnp.maximum(spread(jnp.max(scores, axis=1, keepdims=True)), pu)
        e = jnp.exp(pu - m)
        weights = jnp.exp(scores - tile(m, 6))
        totals = spread(jnp.sum(weights, axis=1, keepdims=True)) + e * rep(s_s[coarse, :], tmp.at[1])
        numerator = nn(weights.astype(bf16), v_win) + e * rep(acc_s[coarse, :], tmp.at[2])
        inverse = 1.0 / totals
        attended = numerator * inverse
        ag_ref[rows, 0:HD] = attended.astype(bf16)
        gf = g.astype(f32)
        delta = spread(jnp.sum(gf * attended, axis=1, keepdims=True))
        shares = weights * tile(inverse, 6)
        prod = nt(g, v_win)
        grads = (shares * (prod - tile(delta, 6)) * SCALE).astype(bf16)
        gq0[rows, :] = nn(grads, k_win)
        gkx[window, 0:HD] += tn(grads, q)
        gkx[window, HD : 2 * HD] += tn(shares.astype(bf16), g)
        scaled = e * inverse
        po_s[coarse, :] = pair_sum(scaled * gf, tmp.at[3])
        pd_s[coarse, :] = pair_sum(scaled * delta, tmp.at[4])
        return carry

    lax.fori_loop(0, CHUNK_BLOCKS, near, 0)

    each_block(level_up, 1)
    each_block(level_up, 2)
    for l in range(3, LEVELS + 1):
        level_up(l, OFF[l], COUNT[l], SIB[l], OFF[l + 1] if l < LEVELS else 0)

    for l in range(LEVELS - 1, 0, -1):
        n = min(COUNT[l], BLOCK)
        for b in range(COUNT[l] // n):
            src = OFF[l + 1] + b * (n // 2)
            rows = slice(OFF[l] + b * n, OFF[l] + (b + 1) * n)
            gq_s[rows, :] += rep(gq_s[src : src + n // 2, :] * 0.5, tmp.at[b % 5])
    for j in range(4):
        own = gs.at[SIB[1] + (j ^ 1) * BLOCK : SIB[1] + ((j ^ 1) + 1) * BLOCK]
        i = j // 2
        above = SIB[2] + (i ^ 1) * BLOCK + (j % 2) * half
        own[...] += rep_pair(gs[above : above + half, :] * 0.5, tmp.at[0], tmp.at[1])

    def finish(b, carry):
        rows = pl.ds(pl.multiple_of(b * BLOCK, BLOCK), BLOCK)
        coarse = pl.ds(pl.multiple_of(b * half, half), half)
        ag_ref[rows, HD : 2 * HD] = (gq0[rows, :] + rep(gq_s[coarse, :] * 0.5, tmp.at[0])).astype(bf16)
        j = b // 2
        src = pl.multiple_of(SIB[1] + (j + 1 - 2 * (j % 2)) * BLOCK + (b % 2) * half, half)
        own = pl.ds(pl.multiple_of((b + 1) * BLOCK, BLOCK), BLOCK)
        local = gkx[own, :] + rep_pair(gs[pl.ds(src, half), :] * 0.5, tmp.at[1], tmp.at[2])
        d_ref[rows, :] = local.astype(bf16)
        return carry

    lax.fori_loop(0, CHUNK_BLOCKS, finish, 0)
    down_ref[...] = gkx[0:BLOCK, :].astype(bf16)
    up_ref[...] = gkx[BLOCK + ROWS :, :].astype(bf16)
    w1_ref[...] = gs[SIB[3] : SIB[3] + BLOCK, :]
    w2_ref[...] = gs[SIB[4] : SIB[4] + BLOCK, :]
    t1_ref[...] = gs[SIB[5] : SIB[5] + BLOCK, :].astype(bf16)
    t2_ref[...] = gs[SIB[6] : SIB[6] + half, :].astype(bf16)
    t3_ref[...] = gs[SIB[6] + half : SIB[6] + BLOCK, :].astype(bf16)


def fold_kernel(r1_ref, r2_ref, r3_ref, w1_ref, w2_ref, own_ref, z1_ref, z2_ref, z3_ref, tmp):
    def rep2(x):
        return rep_pair(x * 0.5, tmp.at[0], tmp.at[1])

    half = BLOCK // 2
    g5 = r1_ref[...].astype(f32) + rep2(r2_ref[...].astype(f32) + r3_ref[...].astype(f32))
    own_ref[...] = g5[0:64, :]
    z1_ref[...] = (w1_ref[...] + rep2(rep2(g5[64:128, :]))).astype(bf16)
    z2_ref[...] = (w2_ref[0:half, :] + rep2(g5[128:192, :])).astype(bf16)
    z3_ref[...] = (w2_ref[half:BLOCK, :] + rep2(g5[192:256, :])).astype(bf16)


def combine_kernel(d_ref, before_ref, after_ref, z1_ref, z2_ref, z3_ref, own_ref, o_ref, tmp, a_s, b_s):
    def rep2(x):
        return rep_pair(x * 0.5, tmp.at[0], tmp.at[1])

    g4 = z2_ref[...].astype(f32) + z3_ref[...].astype(f32) + rep2(own_ref[...])
    g3 = z1_ref[...].astype(f32) + rep2(g4)
    half = BLOCK // 2
    for b in range(2):
        a_s[b * BLOCK : (b + 1) * BLOCK, :] = rep2(g3[b * half : (b + 1) * half, :])
    for b in range(4):
        b_s[b * BLOCK : (b + 1) * BLOCK, :] = rep2(a_s[b * half : (b + 1) * half, :])
    for b in range(8):
        total = d_ref[b * BLOCK : (b + 1) * BLOCK, :].astype(f32) + rep2(b_s[b * half : (b + 1) * half, :])
        if b == 0:
            total = total + before_ref[...].astype(f32)
        if b == 7:
            total = total + after_ref[...].astype(f32)
        o_ref[b * BLOCK : (b + 1) * BLOCK, :] = total.astype(bf16)


def shape(dtype, *dims):
    return jax.ShapeDtypeStruct(dims, dtype)


def call(kernel, out_shape, scalars, args, scratch=(), flops=0, near=()):
    args = [pltpu.with_memory_space_constraint(a, pltpu.VMEM) if i in near else a for i, a in enumerate(args)]
    nbytes = sum(a.size * a.dtype.itemsize for a in args)
    return pl.pallas_call(
        kernel,
        out_shape=out_shape,
        in_specs=[SMEM] * scalars + [VMEM] * (len(args) - scalars),
        out_specs=jax.tree.map(lambda _: VMEM, out_shape),
        scratch_shapes=list(scratch),
        cost_estimate=pl.CostEstimate(flops=flops, bytes_accessed=2 * nbytes, transcendentals=0),
    )(*args)


def per_device(queries, key_rows, value_rows, cotangent):
    own_rows, width = queries.shape
    heads = width // HD
    chunk = (lax.axis_index("y") * lax.axis_size("zh") + lax.axis_index("zh")).astype(jnp.int32).reshape(1)
    wide = 2 * HD

    def swap(x):
        return lax.all_to_all(x, ("zl", "h"), split_axis=0, concat_axis=0, tiled=True)

    def shift(x, distance):
        pairs = [(i, i + distance) for i in range(16) if 0 <= i + distance < 16]
        return lax.ppermute(x, ("y", "zh"), pairs)

    def flip(x, axis, bits):
        return lax.ppermute(x, axis, [(i, i ^ bits) for i in range(4)])

    kv = swap(pack(key_rows, value_rows)).reshape(ROWS, wide)
    l1, l2, l3, l4 = call(
        levels_kernel,
        (shape(bf16, 1024, wide), shape(bf16, 512, wide), shape(bf16, 256, wide), shape(bf16, 128, wide)),
        0,
        (kv,),
        near=(0,),
    )
    z1, z2, z3 = flip(l3, "zh", 1), flip(l4, "zh", 2), flip(l4, "zh", 3)
    before = shift(kv[ROWS - BLOCK :], 1)
    after = shift(kv[:BLOCK], -1)
    qg = swap(pack(queries, cotangent)).reshape(ROWS, wide)
    group = call(group_kernel, shape(bf16, BLOCK, wide), 0, (l4, z1, z2, z3))
    far = lax.all_gather(group, "y")
    coarse = pltpu.VMEM((COARSE_ROWS, HD), f32)
    ag, d, up, down, w1, w2, t1, t2, t3 = call(
        main_kernel,
        (
            shape(bf16, ROWS, wide),
            shape(bf16, ROWS, wide),
            shape(bf16, BLOCK, wide),
            shape(bf16, BLOCK, wide),
            shape(f32, BLOCK, wide),
            shape(f32, BLOCK, wide),
            shape(bf16, BLOCK, wide),
            shape(bf16, 128, wide),
            shape(bf16, 128, wide),
        ),
        1,
        (chunk, kv, qg, l1, l2, before, after, z1, z2, z3, far),
        scratch=(
            pltpu.VMEM((ROWS + 2 * BLOCK, wide), bf16),
            pltpu.VMEM((ROWS + 2 * BLOCK, wide), f32),
            pltpu.VMEM((COARSE_ROWS, HD), bf16),
            pltpu.VMEM((SIB_ROWS, wide), bf16),
            pltpu.VMEM((SIB_ROWS, wide), f32),
            pltpu.VMEM((COARSE_ROWS, wide), f32),
            coarse,
            coarse,
            coarse,
            coarse,
            coarse,
            coarse,
            coarse,
            pltpu.VMEM((ROWS, HD), f32),
            pltpu.VMEM((5, BLOCK + 8, HD), f32),
        ),
        flops=4_000_000_000,
        near=(2,),
    )
    out_ag = swap(ag.reshape(heads, own_rows, wide))
    r1, r2, r3 = flip(t1, "y", 1), flip(t2, "y", 2), flip(t3, "y", 3)
    before = shift(up, 1)
    after = shift(down, -1)
    two = pltpu.VMEM((2, BLOCK + 8, HD), f32)
    own5, w1, w2, w3 = call(
        fold_kernel,
        (shape(f32, 64, wide), shape(bf16, BLOCK, wide), shape(bf16, 128, wide), shape(bf16, 128, wide)),
        0,
        (r1, r2, r3, w1, w2),
        scratch=(two,),
        near=(0, 1, 2),
    )
    z1, z2, z3 = flip(w1, "zh", 1), flip(w2, "zh", 2), flip(w3, "zh", 3)
    gkv = call(
        combine_kernel,
        shape(bf16, ROWS, wide),
        0,
        (d, before, after, z1, z2, z3, own5),
        scratch=(two, pltpu.VMEM((512, wide), f32), pltpu.VMEM((1024, wide), f32)),
        near=(1, 2, 3, 4, 5),
    )
    out_kv = swap(gkv.reshape(heads, own_rows, wide))
    attended, grad_query = unpack(out_ag)
    grad_key, grad_value = unpack(out_kv)
    return attended, grad_query, grad_key, grad_value


def solution(mesh):
    grid = Mesh(mesh.devices.reshape(4, 4, 4, 8), ("y", "zh", "zl", "h"))
    spec = P(("y", "zh", "zl", "h"), None)

    return jax.shard_map(per_device, mesh=grid, in_specs=(spec,) * 4, out_specs=(spec,) * 4, check_vma=False)
```
